32 devices in a mesh: groups: 2 (over x), tm: 8 (over z, y), space: 2 (over core).
Axes of the slice: x: 2, y: 2, z: 4, core: 2. Of those that a mesh axis runs over, the one named last changes fastest.
Arguments:
- queries: bfloat16 [16, 768, 2240], P(('groups', 'tm'), 'space'), parts along dimension 0, may hold values from -6 to 6
- keys: bfloat16 [16, 768, 2240], P(('groups', 'tm'), 'space'), parts along dimension 0, may hold values from -6 to 6
- values: bfloat16 [16, 768, 2240], P(('groups', 'tm'), 'space'), parts along dimension 0, may hold values from -60 to 60
- out_weight: bfloat16 [2240, 2240], P('space'), may hold values from -0.125 to 0.125
- block_len: int32 [16], P(('groups', 'tm')), parts along dimension 0, may hold values from 1 to 768, 4608 in all
Outputs:
- mixed: bfloat16 [16, 768, 2240], P(('groups', 'tm'), 'space'), parts along dimension 0
The draws below stay inside these ranges and needn't reach their ends.
There are 2 independent parts, one for each index of `groups`. The reference program is written for one: setup_inputs(seed, part) draws one part's arguments, and reference() takes and returns one part's arrays. A program takes and returns all parts, laid end to end along the dimension named above; an argument that names none is the same for every part. Nothing has to cross between parts.
Inputs may be any that keep to these rules, and one draw needn't show every extreme that they name: Block b holds block_len[b] live tokens, the first positions of its 768; the 8 lengths of ONE clip sum to 3 * 8 * 768 // 4 (each clip for itself, not all clips together); some block of every clip is full.
All inputs are finite; a program needn't handle non-finite values.
Results may differ from the reference program's by a relative error of at most 0.012.
Values may be sent and summed in bfloat16 or wider, within the bound.
A program may use at most 128 MiB of HBM per device.

```python
import math
import jax
import jax.numpy as jnp
import numpy as np
from jax import lax

D = 2240
HEADS = 20
HEAD_DIM = 112
BLOCKS = 8
SPATIAL = 768


def draw_values(key, part):
    head_index = jnp.arange(HEADS, dtype=jnp.float32) / max(HEADS - 1, 1)
    head_scale = jnp.exp(jnp.log(6.0) * head_index)
    entries = jnp.clip(jax.random.normal(key, (BLOCKS, SPATIAL, HEADS, HEAD_DIM), jnp.float32), -6.0, 6.0)
    scaled = entries * head_scale[None, None, :, None]
    return scaled.reshape(BLOCKS, SPATIAL, HEADS * HEAD_DIM).astype(jnp.bfloat16)


def level_of(key, shape, split, least, high):
    gain = 1.0
    for dim, parts in split:
        draws = jax.random.uniform(jax.random.fold_in(jax.random.fold_in(key, 6), dim), (parts,), jnp.float32, least / len(split), high / len(split))
        gain = gain * jnp.repeat(jnp.exp(draws), shape[dim] // parts).reshape((-1,) + (1,) * (len(shape) - 1 - dim))
    return gain


def length_profile(amount, total, reach, skew):
    weights = [(1 << 20) // math.isqrt(grade ** skew) + 1 for grade in range(2, amount + 1)]
    rest, given = total - reach - (amount - 1), [1] * (amount - 1)
    while rest > 0:
        movable = [i for i in range(amount - 1) if given[i] < reach]
        whole, left = sum([weights[i] for i in movable]), rest
        for i in movable:
            more = min(reach - given[i], max(1, left * weights[i] // whole), rest)
            given[i] = given[i] + more
            rest = rest - more
    return np.array([reach] + given)


def ragged_sizes(stream_key, count, total, bound, lean):
    if count == 2:
        one = jax.random.randint(stream_key, (), max(1, total - bound), min(bound, total - 1) + 1)
        return jnp.stack([one, total - one])
    sizes = jnp.asarray(length_profile(count, total, bound, lean), jnp.int32)
    couples = (count - 1) // 2
    donor, receiver = sizes[1:1 + 2 * couples:2], sizes[2:2 + 2 * couples:2]
    room = jnp.minimum(donor - 1, bound - receiver)
    shifted = jax.random.randint(jax.random.fold_in(stream_key, 1), (couples,), 0, 1 << 20) % (room + 1)
    sizes = sizes.at[1:1 + 2 * couples:2].set(donor - shifted).at[2:2 + 2 * couples:2].set(receiver + shifted)
    return sizes[jax.random.permutation(jax.random.fold_in(stream_key, 2), count)]


def gaussian(stream_key, dims, scale, reach, pieces=(), held_as=jnp.bfloat16):
    gain = level_of(stream_key, dims, pieces, -0.22, 0.18) if pieces else 1.0
    values = jax.random.normal(stream_key, dims, jnp.float32) * scale * gain
    return jnp.minimum(jnp.maximum(values, -reach), reach).astype(held_as)


def setup_inputs(seed: int = 0, part: int = 0) -> dict:
    seeds = jax.random.split(jax.random.key(seed), 6)
    own_keys = jax.random.split(jax.random.fold_in(seeds[5], part), 6)
    return {
        "queries": gaussian(own_keys[0], (BLOCKS, SPATIAL, D), 1.0, 6.0, ((0, 8), (1, 2))),
        "keys": gaussian(own_keys[1], (BLOCKS, SPATIAL, D), 1.0, 6.0, ((0, 8), (1, 2))),
        "values": draw_values(jax.random.fold_in(jax.random.fold_in(seeds[5], part), 71), part),
        "out_weight": gaussian(seeds[3], (D, D), D ** -0.5, 0.125, ((0, 2),)),
        "block_len": ragged_sizes(own_keys[4], BLOCKS, BLOCKS * SPATIAL * 3 // 4, SPATIAL, 0).astype(jnp.int32),
    }


epsilon = 1e-06
norm_epsilon = 1e-06

def reference(queries, keys, values, out_weight, block_len):

    def block_layer(carried, inputs):
        states, key_sums = carried
        query_rows, key_rows, value_rows, length = inputs
        positions = jnp.arange(SPATIAL, dtype=jnp.int32)
        keep_row = (positions < length).astype(jnp.float32)
        key_heads = (jnp.maximum(key_rows.astype(jnp.float32), 0.0) * keep_row[:, None]).reshape(SPATIAL, HEADS, HEAD_DIM)
        value_heads = value_rows.astype(jnp.float32).reshape(SPATIAL, HEADS, HEAD_DIM)
        block_states = jnp.einsum('thi,thj->hij', key_heads, value_heads, precision=lax.Precision.HIGHEST)
        block_sums = lax.optimization_barrier(jnp.sum(key_heads, axis=0))
        whole_states = states + block_states
        whole_sums = key_sums + block_sums
        query_heads = jnp.maximum(query_rows, 0.0).astype(jnp.float32).reshape(SPATIAL, HEADS, HEAD_DIM)
        numerator = jnp.einsum('thi,hij->thj', query_heads, whole_states, precision=lax.Precision.HIGHEST)
        denominator = jnp.einsum('thi,hi->th', query_heads, whole_sums, precision=lax.Precision.HIGHEST) + epsilon
        attended = numerator / denominator[:, :, None] * keep_row[:, None, None]
        mean_square = lax.optimization_barrier(jnp.sum(attended * attended, axis=(1, 2))) / D
        normed = (attended * lax.rsqrt(mean_square + norm_epsilon)[:, None, None]).reshape(SPATIAL, D).astype(jnp.bfloat16)
        output = jnp.dot(normed, out_weight, preferred_element_type=jnp.float32).astype(jnp.bfloat16)
        return ((whole_states, whole_sums), output)
    start_states = jnp.zeros((HEADS, HEAD_DIM, HEAD_DIM), jnp.float32)
    start_sums = jnp.zeros((HEADS, HEAD_DIM), jnp.float32)
    carried, mixed = lax.scan(block_layer, (start_states, start_sums), (queries, keys, values, block_len.astype(jnp.int32)))
    return mixed
```

```python
import functools

import jax
import jax.numpy as jnp
from jax import lax
from jax.experimental import pallas as pl
from jax.experimental.pallas import tpu as pltpu
from jax.sharding import PartitionSpec as P

HEAD_DIM = 112

epsilon = 1e-06
norm_epsilon = 1e-06

TILE = 256
LAG = 3
LOAD_ROWS = 640
SUM_ROWS = 16
CHUNKS = 9
KERNEL_VMEM = 40 << 20


def window_of(tile, width):
    first, last = tile * TILE, min((tile + 1) * TILE, width)
    head_a, head_b = first // HEAD_DIM, (last - 1) // HEAD_DIM
    row_a = head_a * HEAD_DIM // 128 * 128
    row_b = min(-(-(head_b + 1) * HEAD_DIM // 128) * 128, width)
    return first, last, head_a, head_b, row_a, row_b


def spread(piece, zero_of, tile, width):
    first, last, head_a, head_b, row_a, row_b = window_of(tile, width)
    cols = first + lax.broadcasted_iota(jnp.int32, (HEAD_DIM, last - first), 1)
    rows = []
    if head_a * HEAD_DIM > row_a:
        rows.append(zero_of(head_a * HEAD_DIM - row_a))
    for head in range(head_a, head_b + 1):
        inside = (cols >= head * HEAD_DIM) & (cols < (head + 1) * HEAD_DIM)
        rows.append(jnp.where(inside, piece, 0.0).astype(jnp.bfloat16))
    if row_b > (head_b + 1) * HEAD_DIM:
        rows.append(zero_of(row_b - (head_b + 1) * HEAD_DIM))
    return jnp.concatenate(rows, axis=0)


def kernel(
    count,
    q_hbm,
    k_hbm,
    v_hbm,
    w_hbm,
    len_hbm,
    heads,
    scale_ref,
    w,
    q_t,
    k_t,
    v_t,
    q,
    scaled,
    ones,
    part,
    got_core,
    mine,
    y_send,
    got_y,
    z_send,
    got_z,
    other,
    whole,
    local_sem,
    core_sem,
    y_sem,
    z_sem,
    other_sem,
    self_sem,
    relay_sem,
    w_sem,
    load_sem,
    len_ref,
):
    width, tokens = k_t.shape
    half = w_hbm.shape[0]
    tiles = -(-width // TILE)
    per = tiles // part.shape[1]
    chunks = part.shape[1]
    quarter = part.shape[3]
    block = lax.axis_index("tm")
    core = lax.axis_index("space")
    y = lax.rem(block, 2)
    has_left = block >= 2
    has_right = block + 2 < count
    mate = {"space": 1 - core}
    across = {"tm": block + 1 - 2 * y}

    pieces = []
    for first in range(0, width, LOAD_ROWS):
        rows = pl.ds(first, min(LOAD_ROWS, width - first))
        number = len(pieces)
        pair = [
            pltpu.make_async_copy(k_hbm.at[rows], k_t.at[rows], load_sem.at[0, number]),
            pltpu.make_async_copy(v_hbm.at[rows], v_t.at[rows], load_sem.at[1, number]),
        ]
        for load in pair:
            load.start()
        pieces.append(pair)
    w_rows = pl.ds(pl.multiple_of(core * half, 16), half)
    q_load = pltpu.make_async_copy(q_hbm, q_t, local_sem.at[0])
    w_load = pltpu.make_async_copy(w_hbm, w.at[w_rows], local_sem.at[1])

    got_z[...] = jnp.zeros(got_z.shape, got_z.dtype)
    barrier = pltpu.get_barrier_semaphore()
    pl.semaphore_signal(barrier, inc=1, device_id=mate)
    pl.semaphore_signal(barrier, inc=1, device_id=across)

    @pl.when(has_left)
    def _():
        pl.semaphore_signal(barrier, inc=1, device_id={"tm": block - 2})

    @pl.when(has_right)
    def _():
        pl.semaphore_signal(barrier, inc=1, device_id={"tm": block + 2})

    part[:, chunks - 1] = jnp.zeros(part.shape[:1] + part.shape[2:], part.dtype)

    position = core * tokens + lax.broadcasted_iota(jnp.int32, (1, tokens), 1)
    live_row = (position < len_hbm[0]).astype(jnp.bfloat16)
    position = core * tokens + lax.broadcasted_iota(jnp.int32, (tokens, 1), 0)
    live = (position < len_hbm[0]).astype(jnp.float32)

    pl.semaphore_wait(
        barrier, 2 + has_left.astype(jnp.int32) + has_right.astype(jnp.int32)
    )

    def remote(src, dst, sems, j, where):
        return pltpu.make_async_remote_copy(
            src_ref=src, dst_ref=dst, send_sem=sems.at[0, j], recv_sem=sems.at[1, j], device_id=where
        )

    y_copies = []

    def cross(j):
        core_copies[j].wait_recv()
        keep = part[core, j, y].astype(jnp.float32) + got_core[j, y].astype(jnp.float32)
        give = part[core, j, 1 - y].astype(jnp.float32) + got_core[j, 1 - y].astype(jnp.float32)
        y_send[j] = give.astype(jnp.bfloat16)
        copy = remote(y_send.at[j], got_y.at[j], y_sem, j, across)
        copy.start()
        mine[j] = keep
        y_copies.append(copy)

    core_copies = []
    loaded = 0
    contract_tokens = (((1,), (1,)), ((), ()))
    all_ones = jnp.ones((SUM_ROWS, tokens), jnp.bfloat16)
    for j in range(chunks):
        for tile in range(j * per, (j + 1) * per):
            first, last, head_a, head_b, row_a, row_b = window_of(tile, width)
            while loaded * LOAD_ROWS < row_b:
                for load in pieces[loaded]:
                    load.wait()
                begin, end = loaded * LOAD_ROWS, min((loaded + 1) * LOAD_ROWS, width)
                k_t[begin:end] = jnp.maximum(k_t[begin:end], 0.0) * live_row
                loaded += 1
                if loaded == len(pieces):
                    q_load.start()
                    w_load.start()
            product = lax.dot_general(
                k_t[row_a:row_b],
                v_t[first:last],
                contract_tokens,
                preferred_element_type=jnp.float32,
            )
            cols = first + lax.broadcasted_iota(jnp.int32, (HEAD_DIM, last - first), 1)
            state = product[head_a * HEAD_DIM - row_a : (head_a + 1) * HEAD_DIM - row_a]
            for head in range(head_a + 1, head_b + 1):
                start = head * HEAD_DIM - row_a
                state = jnp.where(cols >= head * HEAD_DIM, product[start : start + HEAD_DIM], state)
            sums = lax.dot_general(
                all_ones, k_t[first:last], contract_tokens, preferred_element_type=jnp.float32
            )
            stacked = jnp.concatenate([state, sums], axis=0).astype(jnp.bfloat16)
            at = (tile - j * per) * TILE
            for owner in range(2):
                for side in range(2):
                    row = (2 * owner + side) * quarter
                    part[owner, j, side, :, at : at + last - first] = stacked[row : row + quarter]
        copy = remote(part.at[1 - core, j], got_core.at[j], core_sem, j, mate)
        copy.start()
        core_copies.append(copy)
        if j >= LAG:
            cross(j - LAG)

    w_copy = pltpu.make_async_remote_copy(
        src_ref=w_hbm, dst_ref=w.at[w_rows], send_sem=w_sem.at[0], recv_sem=w_sem.at[1], device_id=mate
    )
    w_copy.start()
    for j in range(max(chunks - LAG, 0), chunks):
        cross(j)

    def prepare():
        for tile in range(tiles):
            first, last, head_a, head_b, row_a, row_b = window_of(tile, width)
            zero_of = lambda rows: jnp.zeros((rows, last - first), jnp.bfloat16)
            ones[tile, : row_b - row_a, : last - first] = spread(
                jnp.ones((HEAD_DIM, last - first), jnp.float32), zero_of, tile, width
            )
        q_load.wait()
        for tile in range(tiles):
            first, last = tile * TILE, min((tile + 1) * TILE, width)
            q[:, first:last] = jnp.maximum(q_t[first:last], 0.0).T

    far = block >= count // 2
    pl.when(far)(prepare)

    y_real = y.astype(jnp.float32)
    other_copies, self_copies = [], []
    for j in range(chunks):
        y_copies[j].wait_recv()
        z_copy = remote(z_send.at[j], got_z.at[j], z_sem, j, {"tm": lax.rem(block + 2, count)})

        @pl.when(has_left)
        def _():
            z_copy.wait_recv()

        earlier = got_z[j].astype(jnp.float32)
        here, there = mine[j], got_y[j].astype(jnp.float32)
        z_send[j] = (earlier + (here + there)).astype(jnp.bfloat16)

        @pl.when(has_right)
        def _():
            z_copy.start()

        other[j] = (earlier + there + (1.0 - y_real) * here).astype(jnp.bfloat16)
        copy = remote(other.at[j], whole.at[core, y, j], other_sem, j, across)
        copy.start()
        other_copies.append(copy)
        whole[core, y, j] = (earlier + here + y_real * there).astype(jnp.bfloat16)
        copy = remote(whole.at[core, y, j], whole.at[core, y, j], self_sem, j, mate)
        copy.start()
        self_copies.append(copy)

    pl.when(jnp.logical_not(far))(prepare)

    def compact(tile):
        first, last = tile * TILE, min((tile + 1) * TILE, width)
        j, at = tile // per, tile % per * TILE
        return jnp.concatenate(
            [whole[o, s, j, :, at : at + last - first] for o in range(2) for s in range(2)], axis=0
        )

    relay_copies = []

    def relay(j):
        other_copies[j].wait_recv()
        slot = whole.at[core, 1 - y, j]
        copy = remote(slot, slot, relay_sem, j, mate)
        copy.start()
        relay_copies.append(copy)

    ready = 0
    squares = jnp.zeros((tokens, 1), jnp.float32)
    for tile in range(tiles):
        first, last, head_a, head_b, row_a, row_b = window_of(tile, width)
        while ready * TILE < row_b:
            if ready % per == 0:
                while len(relay_copies) < min(ready // per + 1 + LAG, chunks):
                    relay(len(relay_copies))
                self_copies[ready // per].wait_recv()
                relay_copies[ready // per].wait_recv()
            begin, end = ready * TILE, min((ready + 1) * TILE, width)
            sums = compact(ready)[HEAD_DIM : HEAD_DIM + SUM_ROWS].astype(jnp.float32)[0:1]
            scaled[:, begin:end] = (q[:, begin:end].astype(jnp.float32) * sums).astype(jnp.bfloat16)
            ready += 1
        zero_of = lambda rows: jnp.zeros((rows, last - first), jnp.bfloat16)
        states = spread(compact(tile)[:HEAD_DIM].astype(jnp.float32), zero_of, tile, width)
        numerator = jnp.dot(q[:, row_a:row_b], states, preferred_element_type=jnp.float32)
        denominator = jnp.dot(
            scaled[:, row_a:row_b],
            ones[tile, : row_b - row_a, : last - first],
            preferred_element_type=jnp.float32,
        )
        attended = numerator / (denominator + epsilon)
        squares = squares + jnp.sum(attended * attended, axis=1, keepdims=True)
        heads[:, first:last] = attended.astype(jnp.bfloat16)
    scale_ref[...] = live * lax.rsqrt(live * squares / width + norm_epsilon)

    w_load.wait()
    w_copy.wait_recv()
    w_copy.wait_send()
    for copy in core_copies + y_copies + other_copies + self_copies + relay_copies:
        copy.wait_send()

    @pl.when(has_right)
    def _():
        for j in range(chunks):
            remote(
                z_send.at[j], got_z.at[j], z_sem, j, {"tm": lax.rem(block + 2, count)}
            ).wait_send()


def project(heads, scale, w, o_hbm, o_t, out_sem):
    width = w.shape[0]
    stores = []
    for tile in range(-(-width // TILE)):
        first, last = tile * TILE, min((tile + 1) * TILE, width)
        product = jnp.dot(heads[...], w[:, first:last], preferred_element_type=jnp.float32)
        o_t[first:last] = (product * scale[...]).astype(jnp.bfloat16).T
        store = pltpu.make_async_copy(o_t.at[first:last], o_hbm.at[first:last], out_sem.at[tile])
        store.start()
        stores.append(store)
    for store in stores:
        store.wait()


def shards(queries, keys, values, out_weight, block_len):
    tokens, width = keys.shape[1:]
    count = lax.axis_size("tm")
    tiles = -(-width // TILE)
    chunks = CHUNKS if tiles % CHUNKS == 0 else tiles
    cols = tiles // chunks * TILE
    quarter = (HEAD_DIM + SUM_ROWS) // 4
    bf16, f32 = jnp.bfloat16, jnp.float32
    piece = (chunks, quarter, cols)
    anywhere = pl.BlockSpec(memory_space=pl.ANY)
    pairs = pltpu.SemaphoreType.DMA((2, chunks))
    onchip = pl.BlockSpec(memory_space=pltpu.VMEM)
    state = pl.pallas_call(
        functools.partial(kernel, count),
        out_shape=[
            pltpu.VMEM((tokens, width), bf16),
            pltpu.VMEM((tokens, 1), f32),
            pltpu.VMEM((width, width), bf16),
        ],
        in_specs=[pl.BlockSpec(memory_space=pltpu.HBM)] * 4 + [pl.BlockSpec(memory_space=pltpu.SMEM)],
        out_specs=[onchip] * 3,
        scratch_shapes=[
            pltpu.VMEM((width, tokens), bf16),
            pltpu.VMEM((width, tokens), bf16),
            pltpu.VMEM((width, tokens), bf16),
            pltpu.VMEM((tokens, width), bf16),
            pltpu.VMEM((tokens, width), bf16),
            pltpu.VMEM((tiles, 512, TILE), bf16),
            pltpu.VMEM((2, chunks, 2, quarter, cols), bf16),
            pltpu.VMEM((chunks, 2, quarter, cols), bf16),
            pltpu.VMEM(piece, f32),
            pltpu.VMEM(piece, bf16),
            pltpu.VMEM(piece, bf16),
            pltpu.VMEM(piece, bf16),
            pltpu.VMEM(piece, bf16),
            pltpu.VMEM(piece, bf16),
            pltpu.VMEM((2, 2) + piece, bf16),
            pltpu.SemaphoreType.DMA((3,)),
            pairs,
            pairs,
            pairs,
            pairs,
            pairs,
            pairs,
            pltpu.SemaphoreType.DMA((2,)),
            pltpu.SemaphoreType.DMA((2, -(-width // LOAD_ROWS))),
            pltpu.SMEM((1,), jnp.int32),
        ],
        compiler_params=pltpu.CompilerParams(
            collective_id=0, has_side_effects=True, vmem_limit_bytes=KERNEL_VMEM
        ),
    )(
        *[
            pltpu.with_memory_space_constraint(array, pltpu.HBM)
            for array in (queries[0].T, keys[0].T, values[0].T, out_weight)
        ],
        block_len,
    )
    mixed = pl.pallas_call(
        project,
        out_shape=jax.ShapeDtypeStruct((width, tokens), bf16),
        in_specs=[onchip] * 3,
        out_specs=anywhere,
        scratch_shapes=[pltpu.VMEM((width, tokens), bf16), pltpu.SemaphoreType.DMA((tiles,))],
        compiler_params=pltpu.CompilerParams(vmem_limit_bytes=KERNEL_VMEM),
    )(*[pltpu.with_memory_space_constraint(array, pltpu.VMEM) for array in state])
    return mixed.T[None]


def solution(mesh):
    in_specs = (
        P(("groups", "tm"), "space", None),
        P(("groups", "tm"), "space", None),
        P(("groups", "tm"), "space", None),
        P("space", None),
        P(("groups", "tm")),
    )
    out_specs = P(("groups", "tm"), "space", None)
    return jax.shard_map(shards, mesh=mesh, in_specs=in_specs, out_specs=out_specs, check_vma=False)
```

```python
import functools

import jax
import jax.numpy as jnp
from jax import lax
from jax.experimental import pallas as pl
from jax.experimental.pallas import tpu as pltpu
from jax.sharding import PartitionSpec as P

HEAD_DIM = 112
SPAN = 2 * HEAD_DIM
TILE = 256

epsilon = 1e-06
norm_epsilon = 1e-06

GROUP = 4
ROWS = 16
CHUNKS = (2, 3, 5)
KERNEL_VMEM = 40 << 20


def chunk_bounds(pairs):
    sizes = CHUNKS if sum(CHUNKS) == pairs else (1,) * pairs
    ends = [sum(sizes[: i + 1]) for i in range(len(sizes))]
    return list(zip([0] + ends[:-1], ends))


def kernel(
    count,
    bounds,
    q_hbm,
    k_hbm,
    v_hbm,
    w_hbm,
    length,
    heads,
    scale_ref,
    w,
    partial,
    q_t,
    k_t,
    v_t,
    q,
    part,
    got_core,
    summed,
    got,
    prefix,
    got_left,
    whole,
    core_sem,
    scatter_sem,
    left_sem,
    gather_sem,
    relay_sem,
    w_load_sem,
    w_sem,
    k_sem,
    v_sem,
    q_sem,
):
    width, tokens = k_t.shape
    pairs = width // SPAN
    half = pairs // 2
    bf16, f32 = jnp.bfloat16, jnp.float32
    block = lax.axis_index("tm")
    core = lax.axis_index("space")
    rank = lax.rem(block, GROUP)
    base = block - rank
    has_left = base > 0
    has_right = base + GROUP < count
    mate = {"space": 1 - core}
    right = {"tm": lax.rem(block + GROUP, count)}
    partners = [GROUP - 1 - rank, lax.rem(rank + 2, GROUP), rank + 1 - 2 * lax.rem(rank, 2)]

    loads = []
    for p in range(pairs):
        rows = pl.ds(p * SPAN, SPAN)
        pair = [
            pltpu.make_async_copy(k_hbm.at[rows], k_t.at[rows], k_sem.at[p]),
            pltpu.make_async_copy(v_hbm.at[rows], v_t.at[p, pl.ds(0, SPAN)], v_sem.at[p]),
        ]
        for load in pair:
            load.start()
        loads.append(pair)
    q_load = pltpu.make_async_copy(q_hbm, q_t, q_sem)
    w_loads, w_copies = [], []
    for i in range(half):
        src = w_hbm.at[pl.ds(i * SPAN, SPAN)]
        dst = w.at[pl.ds(pl.multiple_of((core * half + i) * TILE, TILE), SPAN)]
        w_loads.append(pltpu.make_async_copy(src, dst, w_load_sem.at[i]))
        w_copies.append(
            pltpu.make_async_remote_copy(
                src_ref=src, dst_ref=dst, send_sem=w_sem.at[0, i], recv_sem=w_sem.at[1, i], device_id=mate
            )
        )

    got_left[...] = jnp.zeros(got_left.shape, bf16)
    barrier = pltpu.get_barrier_semaphore()
    pl.semaphore_signal(barrier, inc=1, device_id=mate)
    for partner in partners:
        pl.semaphore_signal(barrier, inc=1, device_id={"tm": base + partner})

    @pl.when(has_left)
    def _():
        pl.semaphore_signal(barrier, inc=1, device_id={"tm": block - GROUP})

    @pl.when(has_right)
    def _():
        pl.semaphore_signal(barrier, inc=1, device_id=right)

    part[1, GROUP - 1] = jnp.zeros(part.shape[2:], bf16)
    for p in range(pairs):
        v_t[p, SPAN:] = jnp.ones((TILE - SPAN, tokens), bf16)
    position = core * tokens + lax.broadcasted_iota(jnp.int32, (1, tokens), 1)
    live_row = (position < length[0]).astype(bf16)
    position = core * tokens + lax.broadcasted_iota(jnp.int32, (tokens, 1), 0)
    live = (position < length[0]).astype(f32)
    cols = lax.broadcasted_iota(jnp.int32, (1, TILE), 1)
    first_head = (cols < HEAD_DIM) | (cols == SPAN)
    second_head = ((cols >= HEAD_DIM) & (cols < SPAN)) | (cols == SPAN + 1)

    def remote(src, dst, sems, j, where):
        return pltpu.make_async_remote_copy(
            src_ref=src, dst_ref=dst, send_sem=sems.at[0, j], recv_sem=sems.at[1, j], device_id=where
        )

    def span(j):
        begin, end = bounds[j]
        return pl.ds(begin * TILE, (end - begin) * TILE)

    core_copies, scatter_copies, gather_copies, relay_copies = [], [], [], []

    def scatter(j):
        at = span(j)
        core_copies[j].wait_recv()
        total = part[core, :, :, at].astype(f32) + got_core[:, :, at].astype(f32)
        summed[:, :, at] = total.astype(bf16)
        copies = []
        for step, partner in enumerate(partners):
            copy = remote(
                summed.at[partner, :, at], got.at[rank, :, at], scatter_sem.at[step], j, {"tm": base + partner}
            )
            copy.start()
            copies.append(copy)
        got[rank, :, at] = summed[rank, :, at]
        scatter_copies.append(copies)

    for begin, end in bounds:
        for p in range(begin, end):
            for load in loads[p]:
                load.wait()
        if end == pairs:
            q_load.start()
            for load in w_loads:
                load.start()
        for p in range(begin, end):
            k = jnp.maximum(k_t[p * SPAN : (p + 1) * SPAN], 0.0) * live_row
            product = lax.dot_general(
                k, v_t[p], (((1,), (1,)), ((), ())), preferred_element_type=f32
            )
            state = jnp.where(first_head, product[:HEAD_DIM], product[HEAD_DIM:]).astype(bf16)
            for number in range(HEAD_DIM // ROWS):
                part[number // GROUP, number % GROUP, :, p * TILE : (p + 1) * TILE] = state[
                    number * ROWS : (number + 1) * ROWS
                ]
    pl.semaphore_wait(
        barrier, GROUP + has_left.astype(jnp.int32) + has_right.astype(jnp.int32)
    )

    for j in range(len(bounds)):
        at = span(j)
        copy = remote(part.at[1 - core, :, :, at], got_core.at[:, :, at], core_sem, j, mate)
        copy.start()
        core_copies.append(copy)
    for j in range(len(bounds)):
        scatter(j)

    for copy in w_copies:
        copy.start()

    def prepare():
        for p in range(pairs):
            w[p * TILE + SPAN : (p + 1) * TILE] = jnp.zeros((TILE - SPAN, width), bf16)
        q_load.wait()
        for p in range(pairs):
            q[:, p * TILE : p * TILE + SPAN] = jnp.maximum(q_t[p * SPAN : (p + 1) * SPAN], 0.0).T

    pl.when(has_left)(prepare)

    def left(j):
        at = span(j)
        return remote(prefix.at[GROUP - 1, :, at], got_left.at[:, at], left_sem, j, right)

    for j in range(len(bounds)):
        at = span(j)
        for copy in scatter_copies[j]:
            copy.wait_recv()

        @pl.when(has_left)
        def _():
            left(j).wait_recv()

        running = got_left[:, at].astype(f32)
        for member in range(GROUP):
            running = running + got[member, :, at].astype(f32)
            prefix[member, :, at] = running.astype(bf16)

        @pl.when(has_right)
        def _():
            left(j).start()

        copies = []
        for step, partner in enumerate(partners):
            copy = remote(
                prefix.at[partner, :, at], whole.at[core, rank, :, at], gather_sem.at[step], j, {"tm": base + partner}
            )
            copy.start()
            copies.append(copy)
        whole[core, rank, :, at] = prefix[rank, :, at]
        gather_copies.append(copies)

    pl.when(jnp.logical_not(has_left))(prepare)

    def relay(j):
        at = span(j)
        for copy in gather_copies[j]:
            copy.wait_recv()
        copy = remote(whole.at[core, :, :, at], whole.at[core, :, :, at], relay_sem, j, mate)
        copy.start()
        relay_copies.append(copy)

    first_mask, second_mask = first_head.astype(bf16), second_head.astype(bf16)
    squares = jnp.zeros((tokens, TILE // 2), f32)
    for j, (begin, end) in enumerate(bounds):
        if j == 0:
            relay(j)
        relay_copies[j].wait_recv()
        for p in range(begin, end):
            at = slice(p * TILE, (p + 1) * TILE)
            states = jnp.concatenate(
                [whole[i // GROUP, i % GROUP, :, at] for i in range(HEAD_DIM // ROWS)], axis=0
            )
            states = jnp.concatenate([states * first_mask, states * second_mask], axis=0)
            product = jnp.dot(q[:, p * TILE : p * TILE + SPAN], states, preferred_element_type=f32)
            inverse = 1.0 / (product[:, TILE // 2 :] + epsilon)
            sums_at = SPAN - TILE // 2
            attended = product * jnp.where(
                cols < HEAD_DIM,
                inverse[:, sums_at : sums_at + 1],
                jnp.where(cols < SPAN, inverse[:, sums_at + 1 : sums_at + 2], 0.0),
            )
            squares = squares + attended[:, : TILE // 2] * attended[:, : TILE // 2]
            squares = squares + attended[:, TILE // 2 :] * attended[:, TILE // 2 :]
            heads[:, at] = attended.astype(bf16)
        if j + 1 < len(bounds):
            relay(j + 1)
            if j == 0:
                for load in w_loads:
                    load.wait()
                for copy in w_copies:
                    copy.wait_recv()
            inner = slice(begin * TILE, end * TILE)
            for first in range(0, width, TILE):
                outer = slice(first, min(first + TILE, width))
                product = jnp.dot(heads[:, inner], w[inner, outer], preferred_element_type=f32)
                partial[:, outer] = product if j == 0 else partial[:, outer] + product
    mean = jnp.sum(squares, axis=1, keepdims=True) / width
    scale_ref[...] = live * lax.rsqrt(live * mean + norm_epsilon)

    for copy in w_copies:
        copy.wait_send()
    for copy in sum(scatter_copies + gather_copies, core_copies + relay_copies):
        copy.wait_send()

    @pl.when(has_right)
    def _():
        for j in range(len(bounds)):
            left(j).wait_send()


def project(begin, heads, scale, w, partial, o_hbm, o_t, out_sem):
    width = w.shape[1]
    stores = []
    for tile in range(-(-width // TILE)):
        first, last = tile * TILE, min((tile + 1) * TILE, width)
        product = jnp.dot(heads[:, begin:], w[begin:, first:last], preferred_element_type=jnp.float32)
        product = product + partial[:, first:last]
        o_t[first:last] = (product * scale[...]).astype(jnp.bfloat16).T
        store = pltpu.make_async_copy(o_t.at[first:last], o_hbm.at[first:last], out_sem.at[tile])
        store.start()
        stores.append(store)
    for store in stores:
        store.wait()


def shards(queries, keys, values, out_weight, block_len):
    tokens, width = keys.shape[1:]
    count = lax.axis_size("tm")
    pairs = width // SPAN
    padded = pairs * TILE
    bounds = chunk_bounds(pairs)
    bf16, f32 = jnp.bfloat16, jnp.float32
    dma = pltpu.SemaphoreType.DMA
    onchip = pl.BlockSpec(memory_space=pltpu.VMEM)
    pieces = (GROUP, ROWS, padded)
    state = pl.pallas_call(
        functools.partial(kernel, count, bounds),
        out_shape=[
            pltpu.VMEM((tokens, padded), bf16),
            pltpu.VMEM((tokens, 1), f32),
            pltpu.VMEM((padded, width), bf16),
            pltpu.VMEM((tokens, width), f32),
        ],
        in_specs=[pl.BlockSpec(memory_space=pltpu.HBM)] * 4 + [pl.BlockSpec(memory_space=pltpu.SMEM)],
        out_specs=[onchip] * 4,
        scratch_shapes=[
            pltpu.VMEM((width, tokens), bf16),
            pltpu.VMEM((width, tokens), bf16),
            pltpu.VMEM((pairs, TILE, tokens), bf16),
            pltpu.VMEM((tokens, padded), bf16),
            pltpu.VMEM((2,) + pieces, bf16),
            pltpu.VMEM(pieces, bf16),
            pltpu.VMEM(pieces, bf16),
            pltpu.VMEM(pieces, bf16),
            pltpu.VMEM(pieces, bf16),
            pltpu.VMEM((ROWS, padded), bf16),
            pltpu.VMEM((2,) + pieces, bf16),
            dma((2, len(bounds))),
            dma((GROUP - 1, 2, len(bounds))),
            dma((2, len(bounds))),
            dma((GROUP - 1, 2, len(bounds))),
            dma((2, len(bounds))),
            dma((pairs // 2,)),
            dma((2, pairs // 2)),
            dma((pairs,)),
            dma((pairs,)),
            dma,
        ],
        compiler_params=pltpu.CompilerParams(
            collective_id=0, has_side_effects=True, vmem_limit_bytes=KERNEL_VMEM
        ),
    )(
        *[
            pltpu.with_memory_space_constraint(array, pltpu.HBM)
            for array in (queries[0].T, keys[0].T, values[0].T, out_weight)
        ],
        block_len,
    )
    mixed = pl.pallas_call(
        functools.partial(project, bounds[-1][0] * TILE),
        out_shape=jax.ShapeDtypeStruct((width, tokens), bf16),
        in_specs=[onchip] * 4,
        out_specs=pl.BlockSpec(memory_space=pl.ANY),
        scratch_shapes=[pltpu.VMEM((width, tokens), bf16), dma((-(-width // TILE),))],
        compiler_params=pltpu.CompilerParams(vmem_limit_bytes=KERNEL_VMEM),
    )(*[pltpu.with_memory_space_constraint(array, pltpu.VMEM) for array in state])
    return mixed.T[None]


def solution(mesh):
    in_specs = (
        P(("groups", "tm"), "space", None),
        P(("groups", "tm"), "space", None),
        P(("groups", "tm"), "space", None),
        P("space", None),
        P(("groups", "tm")),
    )
    out_specs = P(("groups", "tm"), "space", None)
    return jax.shard_map(shards, mesh=mesh, in_specs=in_specs, out_specs=out_specs, check_vma=False)
```

```python
import functools

import jax
import jax.numpy as jnp
from jax import lax
from jax.experimental import pallas as pl
from jax.experimental.pallas import tpu as pltpu
from jax.sharding import PartitionSpec as P

HEAD_DIM = 112
SPAN = 2 * HEAD_DIM
TILE = 256
SPARE = TILE - SPAN

epsilon = 1e-06
norm_epsilon = 1e-06

GROUP = 4
ROWS = 16
CHUNKS = (2, 3, 5)
KERNEL_VMEM = 40 << 20


def chunk_bounds(pairs):
    sizes = CHUNKS if sum(CHUNKS) == pairs else (1,) * pairs
    ends = [sum(sizes[: i + 1]) for i in range(len(sizes))]
    return list(zip([0] + ends[:-1], ends))


def kernel(
    count,
    bounds,
    q_hbm,
    k_hbm,
    v_hbm,
    w_hbm,
    length,
    heads,
    scale_ref,
    w,
    partial,
    q_t,
    k_t,
    v_t,
    q,
    part,
    got_core,
    summed,
    got,
    prefix,
    got_left,
    whole,
    core_sem,
    scatter_sem,
    left_sem,
    gather_sem,
    relay_sem,
    w_load_sem,
    w_sem,
    k_sem,
    v_sem,
    q_sem,
):
    width, tokens = k_t.shape
    pairs = width // SPAN
    half = pairs // 2
    bf16, f32 = jnp.bfloat16, jnp.float32
    block = lax.axis_index("tm")
    core = lax.axis_index("space")
    rank = lax.rem(block, GROUP)
    base = block - rank
    has_left = base > 0
    has_right = base + GROUP < count
    mate = {"space": 1 - core}
    right = {"tm": lax.rem(block + GROUP, count)}
    partners = [GROUP - 1 - rank, lax.rem(rank + 2, GROUP), rank + 1 - 2 * lax.rem(rank, 2)]

    got_left[...] = jnp.zeros(got_left.shape, bf16)
    barrier = pltpu.get_barrier_semaphore()
    pl.semaphore_signal(barrier, inc=1, device_id=mate)
    for partner in partners:
        pl.semaphore_signal(barrier, inc=1, device_id={"tm": base + partner})

    @pl.when(has_left)
    def _():
        pl.semaphore_signal(barrier, inc=1, device_id={"tm": block - GROUP})

    @pl.when(has_right)
    def _():
        pl.semaphore_signal(barrier, inc=1, device_id=right)

    loads = []
    for j, (begin, end) in enumerate(bounds):
        rows = pl.ds(begin * SPAN, (end - begin) * SPAN)
        some = pl.ds(begin, end - begin)
        pair = [
            pltpu.make_async_copy(k_hbm.at[rows], k_t.at[rows], k_sem.at[j]),
            pltpu.make_async_copy(v_hbm.at[some], v_t.at[some, pl.ds(0, SPAN)], v_sem.at[j]),
        ]
        for load in pair:
            load.start()
        loads.append(pair)
    q_load = pltpu.make_async_copy(q_hbm, q_t, q_sem)
    w_loads, w_copies = [], []
    moves = [
        (g * SPARE, SPARE, (1 - core) * (g * TILE + SPAN) + core * ((half - 1) * TILE + g * SPARE), SPARE)
        for g in range(SPAN // SPARE)
    ]
    moves += [(i * SPAN, SPAN, (core * half + i - 1) * TILE, TILE) for i in range(1, half)]
    for number, (start, rows, place, unit) in enumerate(moves):
        src = w_hbm.at[pl.ds(start, rows)]
        dst = w.at[pl.ds(pl.multiple_of(place, unit), rows)]
        w_loads.append(pltpu.make_async_copy(src, dst, w_load_sem.at[number]))
        w_copies.append(
            pltpu.make_async_remote_copy(
                src_ref=src,
                dst_ref=dst,
                send_sem=w_sem.at[0, number],
                recv_sem=w_sem.at[1, number],
                device_id=mate,
            )
        )

    part[1, GROUP - 1] = jnp.zeros(part.shape[2:], bf16)
    for p in range(pairs):
        v_t[p, SPAN:] = jnp.ones((TILE - SPAN, tokens), bf16)
    position = core * tokens + lax.broadcasted_iota(jnp.int32, (1, tokens), 1)
    live_row = (position < length[0]).astype(bf16)
    position = core * tokens + lax.broadcasted_iota(jnp.int32, (tokens, 1), 0)
    live = (position < length[0]).astype(f32)
    cols = lax.broadcasted_iota(jnp.int32, (1, TILE), 1)
    first_head = (cols < HEAD_DIM) | (cols == SPAN)
    second_head = ((cols >= HEAD_DIM) & (cols < SPAN)) | (cols == SPAN + 1)

    def remote(src, dst, sems, j, where):
        return pltpu.make_async_remote_copy(
            src_ref=src, dst_ref=dst, send_sem=sems.at[0, j], recv_sem=sems.at[1, j], device_id=where
        )

    def span(j):
        begin, end = bounds[j]
        return pl.ds(begin * TILE, (end - begin) * TILE)

    core_copies, scatter_copies, gather_copies, relay_copies = [], [], [], []

    def scatter(j):
        at = span(j)
        core_copies[j].wait_recv()
        total = part[core, :, :, at].astype(f32) + got_core[:, :, at].astype(f32)
        summed[:, :, at] = total.astype(bf16)
        copies = []
        for step, partner in enumerate(partners):
            copy = remote(
                summed.at[partner, :, at], got.at[rank, :, at], scatter_sem.at[step], j, {"tm": base + partner}
            )
            copy.start()
            copies.append(copy)
        got[rank, :, at] = summed[rank, :, at]
        scatter_copies.append(copies)

    def states(j):
        begin, end = bounds[j]
        for load in loads[j]:
            load.wait()
        if end == pairs:
            q_load.start()
            for load in w_loads:
                load.start()
        for p in range(begin, end):
            k = jnp.maximum(k_t[p * SPAN : (p + 1) * SPAN], 0.0) * live_row
            product = lax.dot_general(
                k, v_t[p], (((1,), (1,)), ((), ())), preferred_element_type=f32
            )
            state = jnp.where(first_head, product[:HEAD_DIM], product[HEAD_DIM:]).astype(bf16)
            for number in range(HEAD_DIM // ROWS):
                part[number // GROUP, number % GROUP, :, p * TILE : (p + 1) * TILE] = state[
                    number * ROWS : (number + 1) * ROWS
                ]

    def cross(j):
        at = span(j)
        copy = remote(part.at[1 - core, :, :, at], got_core.at[:, :, at], core_sem, j, mate)
        copy.start()
        core_copies.append(copy)

    for j in range(len(bounds)):
        states(j)
    pl.semaphore_wait(
        barrier, GROUP + has_left.astype(jnp.int32) + has_right.astype(jnp.int32)
    )
    for j in range(len(bounds)):
        cross(j)
    for j in range(len(bounds)):
        scatter(j)
    for copy in w_copies:
        copy.start()

    def prepare():
        for tile in range(SPAN // SPARE, pairs - 1):
            w[tile * TILE + SPAN : (tile + 1) * TILE] = jnp.zeros((SPARE, width), bf16)
        q_load.wait()
        for p in range(pairs):
            q[:, p * TILE : p * TILE + SPAN] = jnp.maximum(q_t[p * SPAN : (p + 1) * SPAN], 0.0).T

    pl.when(has_left)(prepare)

    def left(j):
        at = span(j)
        return remote(prefix.at[GROUP - 1, :, at], got_left.at[:, at], left_sem, j, right)

    for j in range(len(bounds)):
        at = span(j)
        for copy in scatter_copies[j]:
            copy.wait_recv()

        @pl.when(has_left)
        def _():
            left(j).wait_recv()

        running = got_left[:, at].astype(f32)
        for member in range(GROUP):
            running = running + got[member, :, at].astype(f32)
            prefix[member, :, at] = running.astype(bf16)

        @pl.when(has_right)
        def _():
            left(j).start()

        copies = []
        for step, partner in enumerate(partners):
            copy = remote(
                prefix.at[partner, :, at], whole.at[core, rank, :, at], gather_sem.at[step], j, {"tm": base + partner}
            )
            copy.start()
            copies.append(copy)
        whole[core, rank, :, at] = prefix[rank, :, at]
        gather_copies.append(copies)

    pl.when(jnp.logical_not(has_left))(prepare)

    def relay(j):
        at = span(j)
        for copy in gather_copies[j]:
            copy.wait_recv()
        copy = remote(whole.at[core, :, :, at], whole.at[core, :, :, at], relay_sem, j, mate)
        copy.start()
        relay_copies.append(copy)

    first_mask, second_mask = first_head.astype(bf16), second_head.astype(bf16)
    squares = jnp.zeros((tokens, TILE // 2), f32)
    for j, (begin, end) in enumerate(bounds):
        if j == 0:
            relay(j)
        relay_copies[j].wait_recv()
        for p in range(begin, end):
            at = slice(p * TILE, (p + 1) * TILE)
            states = jnp.concatenate(
                [whole[i // GROUP, i % GROUP, :, at] for i in range(HEAD_DIM // ROWS)], axis=0
            )
            states = jnp.concatenate([states * first_mask, states * second_mask], axis=0)
            product = jnp.dot(q[:, p * TILE : p * TILE + SPAN], states, preferred_element_type=f32)
            inverse = 1.0 / (product[:, TILE // 2 :] + epsilon)
            sums_at = SPAN - TILE // 2
            attended = product * jnp.where(
                cols < HEAD_DIM,
                inverse[:, sums_at : sums_at + 1],
                jnp.where(cols < SPAN, inverse[:, sums_at + 1 : sums_at + 2], 0.0),
            )
            squares = squares + attended[:, : TILE // 2] * attended[:, : TILE // 2]
            squares = squares + attended[:, TILE // 2 :] * attended[:, TILE // 2 :]
            if p == 0:
                spread = attended
                continue
            tile = p - 1
            low, high = attended[:, : TILE // 2], attended[:, TILE // 2 :]
            if tile < SPAN // SPARE:
                start = tile * SPARE // (TILE // 2) * (TILE // 2)
                moved = spread[:, start : start + TILE // 2]
                shift = (TILE // 2 - SPARE - tile * SPARE) % (TILE // 2)
                if shift:
                    moved = pltpu.roll(moved, shift, 1)
                high = jnp.where(cols[:, TILE // 2 :] < SPAN, high, moved)
            heads[:, tile * TILE : tile * TILE + TILE // 2] = low.astype(bf16)
            heads[:, tile * TILE + TILE // 2 : (tile + 1) * TILE] = high.astype(bf16)
        if j + 1 < len(bounds):
            relay(j + 1)
            if j == 0:
                for load in w_loads:
                    load.wait()
                for copy in w_copies:
                    copy.wait_recv()
            inner = slice(max(begin - 1, 0) * TILE, (end - 1) * TILE)
            for first in range(0, width, TILE):
                outer = slice(first, min(first + TILE, width))
                product = jnp.dot(heads[:, inner], w[inner, outer], preferred_element_type=f32)
                partial[:, outer] = product if j == 0 else partial[:, outer] + product
    mean = jnp.sum(squares, axis=1, keepdims=True) / width
    scale_ref[...] = live * lax.rsqrt(live * mean + norm_epsilon)

    for copy in w_copies:
        copy.wait_send()
    for copy in sum(scatter_copies + gather_copies, core_copies + relay_copies):
        copy.wait_send()

    @pl.when(has_right)
    def _():
        for j in range(len(bounds)):
            left(j).wait_send()


def project(begin, heads, scale, w, partial, o_hbm, o_t, out_sem):
    width = w.shape[1]
    stores = []
    for tile in range(-(-width // TILE)):
        first, last = tile * TILE, min((tile + 1) * TILE, width)
        product = jnp.dot(heads[:, begin:], w[begin:, first:last], preferred_element_type=jnp.float32)
        product = product + partial[:, first:last]
        o_t[first:last] = (product * scale[...]).astype(jnp.bfloat16).T
        store = pltpu.make_async_copy(o_t.at[first:last], o_hbm.at[first:last], out_sem.at[tile])
        store.start()
        stores.append(store)
    for store in stores:
        store.wait()


def shards(queries, keys, values, out_weight, block_len):
    tokens, width = keys.shape[1:]
    count = lax.axis_size("tm")
    pairs = width // SPAN
    padded = pairs * TILE
    packed = padded - TILE
    moves = pairs // 2 - 1 + SPAN // SPARE
    bounds = chunk_bounds(pairs)
    bf16, f32 = jnp.bfloat16, jnp.float32
    dma = pltpu.SemaphoreType.DMA
    onchip = pl.BlockSpec(memory_space=pltpu.VMEM)
    pieces = (GROUP, ROWS, padded)
    state = pl.pallas_call(
        functools.partial(kernel, count, bounds),
        out_shape=[
            pltpu.VMEM((tokens, packed), bf16),
            pltpu.VMEM((tokens, 1), f32),
            pltpu.VMEM((packed, width), bf16),
            pltpu.VMEM((tokens, width), f32),
        ],
        in_specs=[pl.BlockSpec(memory_space=pltpu.HBM)] * 4 + [pl.BlockSpec(memory_space=pltpu.SMEM)],
        out_specs=[onchip] * 4,
        scratch_shapes=[
            pltpu.VMEM((width, tokens), bf16),
            pltpu.VMEM((width, tokens), bf16),
            pltpu.VMEM((pairs, TILE, tokens), bf16),
            pltpu.VMEM((tokens, padded), bf16),
            pltpu.VMEM((2,) + pieces, bf16),
            pltpu.VMEM(pieces, bf16),
            pltpu.VMEM(pieces, bf16),
            pltpu.VMEM(pieces, bf16),
            pltpu.VMEM(pieces, bf16),
            pltpu.VMEM((ROWS, padded), bf16),
            pltpu.VMEM((2,) + pieces, bf16),
            dma((2, len(bounds))),
            dma((GROUP - 1, 2, len(bounds))),
            dma((2, len(bounds))),
            dma((GROUP - 1, 2, len(bounds))),
            dma((2, len(bounds))),
            dma((moves,)),
            dma((2, moves)),
            dma((len(bounds),)),
            dma((len(bounds),)),
            dma,
        ],
        compiler_params=pltpu.CompilerParams(
            collective_id=0, has_side_effects=True, vmem_limit_bytes=KERNEL_VMEM
        ),
    )(
        *[
            pltpu.with_memory_space_constraint(array, pltpu.HBM)
            for array in (
                queries[0].T,
                keys[0].T,
                values[0].T.reshape(pairs, SPAN, tokens),
                out_weight,
            )
        ],
        block_len,
    )
    mixed = pl.pallas_call(
        functools.partial(project, (bounds[-1][0] - 1) * TILE),
        out_shape=jax.ShapeDtypeStruct((width, tokens), bf16),
        in_specs=[onchip] * 4,
        out_specs=pl.BlockSpec(memory_space=pl.ANY),
        scratch_shapes=[pltpu.VMEM((width, tokens), bf16), dma((-(-width // TILE),))],
        compiler_params=pltpu.CompilerParams(vmem_limit_bytes=KERNEL_VMEM),
    )(*[pltpu.with_memory_space_constraint(array, pltpu.VMEM) for array in state])
    return mixed.T[None]


def solution(mesh):
    in_specs = (
        P(("groups", "tm"), "space", None),
        P(("groups", "tm"), "space", None),
        P(("groups", "tm"), "space", None),
        P("space", None),
        P(("groups", "tm")),
    )
    out_specs = P(("groups", "tm"), "space", None)
    return jax.shard_map(shards, mesh=mesh, in_specs=in_specs, out_specs=out_specs, check_vma=False)
```

```python
import functools

import jax
import jax.numpy as jnp
from jax import lax
from jax.experimental import pallas as pl
from jax.experimental.pallas import tpu as pltpu
from jax.sharding import PartitionSpec as P

HEAD_DIM = 112
SPAN = 2 * HEAD_DIM
TILE = 256
SPARE = TILE - SPAN

epsilon = 1e-06
norm_epsilon = 1e-06

GROUP = 4
ROWS = 16
CHUNKS = (2, 3, 5)
KERNEL_VMEM = 40 << 20


def chunk_bounds(pairs):
    sizes = CHUNKS if sum(CHUNKS) == pairs else (1,) * pairs
    ends = [sum(sizes[: i + 1]) for i in range(len(sizes))]
    return list(zip([0] + ends[:-1], ends))


def kernel(
    count,
    bounds,
    q_hbm,
    k_hbm,
    v_hbm,
    w_hbm,
    length,
    heads,
    scale_ref,
    w,
    partial,
    q_t,
    k_t,
    v_t,
    q,
    part,
    got_core,
    summed,
    got,
    prefix,
    got_left,
    whole,
    core_sem,
    scatter_sem,
    left_sem,
    gather_sem,
    relay_sem,
    w_load_sem,
    w_sem,
    k_sem,
    v_sem,
    q_sem,
):
    width, tokens = k_t.shape
    pairs = width // SPAN
    half = pairs // 2
    bf16, f32 = jnp.bfloat16, jnp.float32
    block = lax.axis_index("tm")
    core = lax.axis_index("space")
    rank = lax.rem(block, GROUP)
    base = block - rank
    has_left = base > 0
    has_right = base + GROUP < count
    mate = {"space": 1 - core}
    right = {"tm": lax.rem(block + GROUP, count)}
    partners = [GROUP - 1 - rank, lax.rem(rank + 2, GROUP), rank + 1 - 2 * lax.rem(rank, 2)]

    got_left[...] = jnp.zeros(got_left.shape, bf16)
    barrier = pltpu.get_barrier_semaphore()
    pl.semaphore_signal(barrier, inc=1, device_id=mate)
    for partner in partners:
        pl.semaphore_signal(barrier, inc=1, device_id={"tm": base + partner})

    @pl.when(has_left)
    def _():
        pl.semaphore_signal(barrier, inc=1, device_id={"tm": block - GROUP})

    @pl.when(has_right)
    def _():
        pl.semaphore_signal(barrier, inc=1, device_id=right)

    loads = []
    for j, (begin, end) in enumerate(bounds):
        rows = pl.ds(begin * SPAN, (end - begin) * SPAN)
        some = pl.ds(begin, end - begin)
        pair = [
            pltpu.make_async_copy(k_hbm.at[rows], k_t.at[rows], k_sem.at[j]),
            pltpu.make_async_copy(v_hbm.at[some], v_t.at[some, pl.ds(0, SPAN)], v_sem.at[j]),
        ]
        for load in pair:
            load.start()
        loads.append(pair)
    q_load = pltpu.make_async_copy(q_hbm, q_t, q_sem)
    w_loads, w_copies = [], []
    moves = [
        (g * SPARE, SPARE, (1 - core) * (g * TILE + SPAN) + core * ((half - 1) * TILE + g * SPARE), SPARE)
        for g in range(SPAN // SPARE)
    ]
    moves += [(i * SPAN, SPAN, (core * half + i - 1) * TILE, TILE) for i in range(1, half)]
    for number, (start, rows, place, unit) in enumerate(moves):
        src = w_hbm.at[pl.ds(start, rows)]
        dst = w.at[pl.ds(pl.multiple_of(place, unit), rows)]
        w_loads.append(pltpu.make_async_copy(src, dst, w_load_sem.at[number]))
        w_copies.append(
            pltpu.make_async_remote_copy(
                src_ref=src,
                dst_ref=dst,
                send_sem=w_sem.at[0, number],
                recv_sem=w_sem.at[1, number],
                device_id=mate,
            )
        )

    part[1, GROUP - 1] = jnp.zeros(part.shape[2:], bf16)
    for p in range(pairs):
        v_t[p, SPAN:] = jnp.ones((TILE - SPAN, tokens), bf16)
    position = core * tokens + lax.broadcasted_iota(jnp.int32, (1, tokens), 1)
    live_row = (position < length[0]).astype(bf16)
    position = core * tokens + lax.broadcasted_iota(jnp.int32, (tokens, 1), 0)
    live = (position < length[0]).astype(f32)
    cols = lax.broadcasted_iota(jnp.int32, (1, TILE), 1)
    first_head = (cols < HEAD_DIM) | (cols == SPAN)
    second_head = ((cols >= HEAD_DIM) & (cols < SPAN)) | (cols == SPAN + 1)

    def remote(src, dst, sems, j, where):
        return pltpu.make_async_remote_copy(
            src_ref=src, dst_ref=dst, send_sem=sems.at[0, j], recv_sem=sems.at[1, j], device_id=where
        )

    def span(j):
        begin, end = bounds[j]
        return pl.ds(begin * TILE, (end - begin) * TILE)

    core_copies, scatter_copies, gather_copies, relay_copies = [], [], [], []

    def scatter(j):
        at = span(j)
        core_copies[j].wait_recv()
        total = part[core, :, :, at].astype(f32) + got_core[:, :, at].astype(f32)
        summed[:, :, at] = total.astype(bf16)
        copies = []
        for step, partner in enumerate(partners):
            copy = remote(
                summed.at[partner, :, at], got.at[rank, :, at], scatter_sem.at[step], j, {"tm": base + partner}
            )
            copy.start()
            copies.append(copy)
        got[rank, :, at] = summed[rank, :, at]
        scatter_copies.append(copies)

    def states(j):
        begin, end = bounds[j]
        for load in loads[j]:
            load.wait()
        if end == pairs:
            q_load.start()
            for load in w_loads:
                load.start()
        for p in range(begin, end):
            k = jnp.maximum(k_t[p * SPAN : (p + 1) * SPAN], 0.0) * live_row
            product = lax.dot_general(
                k, v_t[p], (((1,), (1,)), ((), ())), preferred_element_type=f32
            )
            state = jnp.where(first_head, product[:HEAD_DIM], product[HEAD_DIM:]).astype(bf16)
            for number in range(HEAD_DIM // ROWS):
                part[number // GROUP, number % GROUP, :, p * TILE : (p + 1) * TILE] = state[
                    number * ROWS : (number + 1) * ROWS
                ]

    def cross(j):
        at = span(j)
        copy = remote(part.at[1 - core, :, :, at], got_core.at[:, :, at], core_sem, j, mate)
        copy.start()
        core_copies.append(copy)

    for j in range(len(bounds)):
        states(j)
    pl.semaphore_wait(
        barrier, GROUP + has_left.astype(jnp.int32) + has_right.astype(jnp.int32)
    )
    for j in range(len(bounds)):
        cross(j)
    for j in range(len(bounds)):
        scatter(j)
    for copy in w_copies:
        copy.start()

    def prepare():
        for tile in range(SPAN // SPARE, pairs - 1):
            w[tile * TILE + SPAN : (tile + 1) * TILE] = jnp.zeros((SPARE, width), bf16)
        q_load.wait()

        @pl.loop(0, pairs)
        def _(p):
            rows = pl.ds(pl.multiple_of(p * SPAN, SPAN), SPAN)
            q[:, pl.ds(pl.multiple_of(p * TILE, TILE), SPAN)] = jnp.maximum(q_t[rows], 0.0).T


    pl.when(has_left)(prepare)

    def left(j):
        at = span(j)
        return remote(prefix.at[GROUP - 1, :, at], got_left.at[:, at], left_sem, j, right)

    for j in range(len(bounds)):
        at = span(j)
        for copy in scatter_copies[j]:
            copy.wait_recv()

        @pl.when(has_left)
        def _():
            left(j).wait_recv()

        running = got_left[:, at].astype(f32)
        for member in range(GROUP):
            running = running + got[member, :, at].astype(f32)
            prefix[member, :, at] = running.astype(bf16)

        @pl.when(has_right)
        def _():
            left(j).start()

        copies = []
        for step, partner in enumerate(partners):
            copy = remote(
                prefix.at[partner, :, at], whole.at[core, rank, :, at], gather_sem.at[step], j, {"tm": base + partner}
            )
            copy.start()
            copies.append(copy)
        whole[core, rank, :, at] = prefix[rank, :, at]
        gather_copies.append(copies)

    pl.when(jnp.logical_not(has_left))(prepare)

    for copy in sum(scatter_copies, core_copies):
        copy.wait_send()

    @pl.when(has_right)
    def _():
        for j in range(len(bounds)):
            left(j).wait_send()

    def relay(j):
        at = span(j)
        for copy in gather_copies[j]:
            copy.wait_recv()
        copy = remote(whole.at[core, :, :, at], whole.at[core, :, :, at], relay_sem, j, mate)
        copy.start()
        relay_copies.append(copy)

    first_mask, second_mask = first_head.astype(bf16), second_head.astype(bf16)
    lanes = cols[:, : TILE // 2]
    squares = jnp.zeros((tokens, TILE // 2), f32)
    for j, (begin, end) in enumerate(bounds):
        if j == 0:
            relay(j)
        relay_copies[j].wait_recv()
        for p in range(begin, end):
            at = slice(p * TILE, (p + 1) * TILE)
            states = jnp.concatenate(
                [whole[i // GROUP, i % GROUP, :, at] for i in range(HEAD_DIM // ROWS)], axis=0
            )
            states = jnp.concatenate([states * first_mask, states * second_mask], axis=0)
            product = jnp.dot(q[:, p * TILE : p * TILE + SPAN], states, preferred_element_type=f32)
            low, high = product[:, : TILE // 2], product[:, TILE // 2 :]
            sums = high + epsilon
            inverse = 1.0 / sums
            sums_at = SPAN - TILE // 2
            first, second = inverse[:, sums_at : sums_at + 1], inverse[:, sums_at + 1 : sums_at + 2]
            low = low * jnp.where(lanes < HEAD_DIM, first, second)
            high = jnp.where(lanes < sums_at, high * second, 0.0)
            squares = squares + (low * low + high * high)
            if p == 0:
                spread = [low, high]
                continue
            tile = p - 1
            if tile < SPAN // SPARE:
                moved = spread[tile * SPARE // (TILE // 2)]
                shift = (TILE // 2 - SPARE - tile * SPARE) % (TILE // 2)
                if shift:
                    moved = pltpu.roll(moved, shift, 1)
                high = jnp.where(lanes < sums_at, high, moved)
            heads[:, tile * TILE : tile * TILE + TILE // 2] = low.astype(bf16)
            heads[:, tile * TILE + TILE // 2 : (tile + 1) * TILE] = high.astype(bf16)
        if j + 1 < len(bounds):
            relay(j + 1)
            if j == 0:
                for load in w_loads:
                    load.wait()
                for copy in w_copies:
                    copy.wait()
            inner = slice(max(begin - 1, 0) * TILE, (end - 1) * TILE)
            for first in range(0, width, TILE):
                outer = slice(first, min(first + TILE, width))
                product = jnp.dot(heads[:, inner], w[inner, outer], preferred_element_type=f32)
                partial[:, outer] = product if j == 0 else partial[:, outer] + product
    mean = jnp.sum(squares, axis=1, keepdims=True) / width
    scale_ref[...] = live * lax.rsqrt(live * mean + norm_epsilon)

    for copy in sum(gather_copies, relay_copies):
        copy.wait_send()


def project(begin, heads, scale, w, partial, o_hbm, o_t, out_sem):
    width = w.shape[1]
    stores = []
    for tile in range(-(-width // TILE)):
        first, last = tile * TILE, min((tile + 1) * TILE, width)
        product = jnp.dot(heads[:, begin:], w[begin:, first:last], preferred_element_type=jnp.float32)
        product = product + partial[:, first:last]
        o_t[first:last] = (product * scale[...]).astype(jnp.bfloat16).T
        store = pltpu.make_async_copy(o_t.at[first:last], o_hbm.at[first:last], out_sem.at[tile])
        store.start()
        stores.append(store)
    for store in stores:
        store.wait()


def shards(queries, keys, values, out_weight, block_len):
    tokens, width = keys.shape[1:]
    count = lax.axis_size("tm")
    pairs = width // SPAN
    padded = pairs * TILE
    packed = padded - TILE
    moves = pairs // 2 - 1 + SPAN // SPARE
    bounds = chunk_bounds(pairs)
    bf16, f32 = jnp.bfloat16, jnp.float32
    dma = pltpu.SemaphoreType.DMA
    onchip = pl.BlockSpec(memory_space=pltpu.VMEM)
    pieces = (GROUP, ROWS, padded)
    state = pl.pallas_call(
        functools.partial(kernel, count, bounds),
        out_shape=[
            pltpu.VMEM((tokens, packed), bf16),
            pltpu.VMEM((tokens, 1), f32),
            pltpu.VMEM((packed, width), bf16),
            pltpu.VMEM((tokens, width), f32),
        ],
        in_specs=[pl.BlockSpec(memory_space=pltpu.HBM)] * 4 + [pl.BlockSpec(memory_space=pltpu.SMEM)],
        out_specs=[onchip] * 4,
        scratch_shapes=[
            pltpu.VMEM((width, tokens), bf16),
            pltpu.VMEM((width, tokens), bf16),
            pltpu.VMEM((pairs, TILE, tokens), bf16),
            pltpu.VMEM((tokens, padded), bf16),
            pltpu.VMEM((2,) + pieces, bf16),
            pltpu.VMEM(pieces, bf16),
            pltpu.VMEM(pieces, bf16),
            pltpu.VMEM(pieces, bf16),
            pltpu.VMEM(pieces, bf16),
            pltpu.VMEM((ROWS, padded), bf16),
            pltpu.VMEM((2,) + pieces, bf16),
            dma((2, len(bounds))),
            dma((GROUP - 1, 2, len(bounds))),
            dma((2, len(bounds))),
            dma((GROUP - 1, 2, len(bounds))),
            dma((2, len(bounds))),
            dma((moves,)),
            dma((2, moves)),
            dma((len(bounds),)),
            dma((len(bounds),)),
            dma,
        ],
        compiler_params=pltpu.CompilerParams(
            collective_id=0, has_side_effects=True, vmem_limit_bytes=KERNEL_VMEM
        ),
    )(
        *[
            pltpu.with_memory_space_constraint(array, pltpu.HBM)
            for array in (
                queries[0].T,
                keys[0].T,
                values[0].T.reshape(pairs, SPAN, tokens),
                out_weight,
            )
        ],
        block_len,
    )
    mixed = pl.pallas_call(
        functools.partial(project, (bounds[-1][0] - 1) * TILE),
        out_shape=jax.ShapeDtypeStruct((width, tokens), bf16),
        in_specs=[onchip] * 4,
        out_specs=pl.BlockSpec(memory_space=pl.ANY),
        scratch_shapes=[pltpu.VMEM((width, tokens), bf16), dma((-(-width // TILE),))],
        compiler_params=pltpu.CompilerParams(vmem_limit_bytes=KERNEL_VMEM),
    )(*[pltpu.with_memory_space_constraint(array, pltpu.VMEM) for array in state])
    return mixed.T[None]


def solution(mesh):
    in_specs = (
        P(("groups", "tm"), "space", None),
        P(("groups", "tm"), "space", None),
        P(("groups", "tm"), "space", None),
        P("space", None),
        P(("groups", "tm")),
    )
    out_specs = P(("groups", "tm"), "space", None)
    return jax.shard_map(shards, mesh=mesh, in_specs=in_specs, out_specs=out_specs, check_vma=False)
```
